128 devices in a mesh: seq: 16 (over x, y), head: 8 (over z, core).
Axes of the slice: x: 4, y: 4, z: 4, core: 2. Of those that a mesh axis runs over, the one named last changes fastest.
Arguments:
- queries: bfloat16 [32768, 8192], P('seq', 'head'), may hold values from -6 to 6
- key_vectors: bfloat16 [32768, 8192], P('seq', 'head'), may hold values from -6 to 6
- value_vectors: bfloat16 [32768, 8192], P('seq', 'head'), may hold values from -6 to 6
- level_weights: float32 [64, 16, 32768], P('head', None, 'seq'), may hold values from 0.22 to 13.45, as said below
- norm_gain: float32 [8192], P('head'), may hold values from 0.25 to 1.75
Outputs:
- normed: bfloat16 [32768, 8192], P('seq', 'head')
The draws below stay inside these ranges and needn't reach their ends.
Inputs may be any that keep to these rules, and one draw needn't show every extreme that they name: `level_weights`: positive.
All inputs are finite; a program needn't handle non-finite values.
Results may differ from the reference program's by a relative error of at most 0.0056.
Values may be sent and summed in bfloat16 or wider, within the bound.
A program may use at most 192 MiB of HBM per device.

```python
import jax
import jax.numpy as jnp
from jax import lax

HEADS = 64
HEAD_DIM = 128
VALUE_DIM = 128
LEVELS = 16
TOK_DEV = 2048
TOKENS = 32768


def draw_level_weights(key, part):
    uniform_draw = jax.random.uniform(key, (HEADS, LEVELS, TOKENS), jnp.float32)
    head_factor = 3.0 ** (jnp.arange(HEADS, dtype=jnp.float32) / (HEADS - 1))
    base_values = jnp.exp(-1.5 + 3.0 * uniform_draw)
    return base_values * head_factor[:, None, None]


def level_of(stream_key, shape, cuts, least, largest):
    def one(position, parts):
        heights = jax.random.uniform(jax.random.fold_in(jax.random.fold_in(stream_key, 6), position), (parts,), jnp.float32, least / len(cuts), largest / len(cuts))
        return jnp.repeat(jnp.exp(heights), shape[position] // parts).reshape((-1,) + (1,) * (len(shape) - position - 1))

    loudness = one(*cuts[0])
    for cut in cuts[1:]:
        loudness = loudness * one(*cut)
    return loudness


def normal_values(key, dims, deviation, most, split=(), held_as=jnp.bfloat16):
    array = deviation * jax.random.normal(key, dims, jnp.float32)
    if split:
        array = array * level_of(key, dims, split, -0.22, 0.18)
    return jnp.clip(array, -most, most).astype(held_as)


def setup_inputs(seed: int = 0) -> dict:
    key_of = jax.random.split(jax.random.key(seed), 6)
    return {
        "queries": normal_values(key_of[0], (TOKENS, HEADS * HEAD_DIM), 1.0, 6.0, ((0, 16), (1, 8))),
        "key_vectors": normal_values(key_of[1], (TOKENS, HEADS * HEAD_DIM), 1.0, 6.0, ((0, 16), (1, 8))),
        "value_vectors": normal_values(key_of[2], (TOKENS, HEADS * VALUE_DIM), 1.0, 6.0, ((0, 16), (1, 8))),
        "level_weights": draw_level_weights(jax.random.fold_in(key_of[5], 71), 0),
        "norm_gain": jnp.clip(1.0 + 0.15 * jax.random.normal(key_of[4], (HEADS * VALUE_DIM,), jnp.float32), 0.25, 1.75),
    }


def bit_length(numbers, count):
    counted = jnp.zeros(numbers.shape, jnp.int32)
    for exponent in range(count):
        counted = counted + (numbers >= 1 << exponent).astype(jnp.int32)
    return counted

def one_head(operands):
    query, key_rows, value_rows, weights = operands
    block_count = TOKENS // TOK_DEV
    scaling = HEAD_DIM ** (-0.5)
    local_bits = TOK_DEV.bit_length() - 1
    cross_bits = block_count.bit_length() - 1
    query_blocks = query.astype(jnp.float32).reshape(block_count, TOK_DEV, HEAD_DIM)
    key_blocks = key_rows.astype(jnp.float32).reshape(block_count, TOK_DEV, HEAD_DIM)
    value_blocks = value_rows.astype(jnp.float32).reshape(block_count, TOK_DEV, VALUE_DIM)
    weight_blocks = weights.reshape(LEVELS, block_count, TOK_DEV)
    row_block = min(TOK_DEV, 512)
    pieces = []
    for start_row in range(0, TOK_DEV, row_block):
        end_row = start_row + row_block
        row_ids = jnp.arange(start_row, end_row, dtype=jnp.int32)
        col_ids = jnp.arange(0, end_row, dtype=jnp.int32)
        levels = bit_length(row_ids[:, None] ^ col_ids[None, :], local_bits)
        scores = jnp.einsum('crd,csd->crs', query_blocks[:, start_row:end_row], key_blocks[:, :end_row]) * scaling
        factors = jnp.zeros(scores.shape, jnp.float32)
        for depth_id in range(local_bits + 1):
            factors = jnp.where(levels[None] == depth_id, weight_blocks[depth_id, :, start_row:end_row][:, :, None], factors)
        causal = (col_ids[None, :] <= row_ids[:, None])[None]
        weighted = jnp.where(causal, scores * factors, 0.0).astype(jnp.bfloat16)
        pieces.append(jnp.einsum('crs,cse->cre', weighted.astype(jnp.float32), value_blocks[:, :end_row]))
    inside = jnp.concatenate(pieces, axis=1)
    states = jnp.einsum('ctd,cte->cde', key_blocks, value_blocks)
    states = lax.optimization_barrier(states.astype(jnp.bfloat16)).astype(jnp.float32)
    prefix = jnp.concatenate([jnp.zeros((1, HEAD_DIM, VALUE_DIM), jnp.float32), jnp.cumsum(states, axis=0)], axis=0)
    block_ids = jnp.arange(block_count, dtype=jnp.int32)
    across = jnp.zeros((block_count, TOK_DEV, VALUE_DIM), jnp.float32)
    for bit_level in range(cross_bits):
        lower = block_ids >> bit_level + 1 << bit_level + 1
        upper = lower + (1 << bit_level)
        present = (block_ids >> bit_level & 1).astype(jnp.float32)
        bucket = (prefix[upper] - prefix[lower]) * present[:, None, None]
        rounded = lax.optimization_barrier(bucket.astype(jnp.bfloat16))
        readout = jnp.einsum('ctd,cde->cte', query_blocks, rounded.astype(jnp.float32)) * scaling
        across = across + weight_blocks[local_bits + 1 + bit_level][:, :, None] * readout
    return (inside + across).reshape(TOKENS, VALUE_DIM)

def reference(queries, key_vectors, value_vectors, level_weights, norm_gain):
    query_heads = queries.reshape(TOKENS, HEADS, HEAD_DIM).transpose(1, 0, 2)
    key_heads = key_vectors.reshape(TOKENS, HEADS, HEAD_DIM).transpose(1, 0, 2)
    value_heads = value_vectors.reshape(TOKENS, HEADS, VALUE_DIM).transpose(1, 0, 2)
    outputs = lax.map(one_head, (query_heads, key_heads, value_heads, level_weights))
    mixture = outputs.transpose(1, 0, 2).reshape(TOKENS, HEADS * VALUE_DIM)
    square = lax.optimization_barrier(jnp.sum(mixture * mixture, axis=1, keepdims=True))
    return (mixture * norm_gain * lax.rsqrt(square / (HEADS * VALUE_DIM) + 1e-05)).astype(jnp.bfloat16)
```

```python
import functools

import jax
import jax.numpy as jnp
from jax import lax
from jax.experimental import pallas as pl
from jax.experimental.pallas import tpu as pltpu
from jax.sharding import PartitionSpec as P

D = 128
E = 128
C = 256
HALF = 128
HEADS = 64
MESH = pl.DeviceIdType.MESH
F32 = jnp.float32
BF16 = jnp.bfloat16


def nt(a, b):
    return lax.dot_general(a, b, (((1,), (1,)), ((), ())), preferred_element_type=F32)


def nn(a, b):
    return lax.dot_general(a, b, (((1,), (0,)), ((), ())), preferred_element_type=F32)


def partner_mask(bit):
    return 1 << bit if bit % 2 == 0 else 3 << (bit - 1)


def buckets_of(chunks):
    table = {}
    bit = 0
    while 1 << bit < chunks:
        for start in range(0, chunks, 2 << bit):
            table[(bit, start)] = len(table)
        bit += 1
    return table


def kernel(
    seq_n, head_n, heads, tokens,
    q_hbm, k_hbm, v_hbm, lam_hbm, gain_ref,
    out_ref,
    q_s, k_s, v_s, lam_s, vt_s, acc_s, lv_s, p_s, send_s, recv_s, sq_s, sqx_s, gcol_s, d_s, g_s,
    load_sem, lam_sem, send_sem, recv_sem, sq_send_sem, sq_recv_sem,
):
    chunks = tokens // C
    bits = seq_n.bit_length() - 1
    local_bits = tokens.bit_length() - 1
    me_seq = lax.axis_index("seq")
    me_head = lax.axis_index("head")
    table = buckets_of(chunks)
    scaling = D ** (-0.5)

    def load(which, h):
        src, dst = ((q_hbm, q_s), (k_hbm, k_s), (v_hbm, v_s))[which]
        cols = pl.ds(pl.multiple_of(h * D, D), D)
        return pltpu.make_async_copy(src.at[:, cols], dst.at[h], load_sem.at[which, h])

    lam_copy = pltpu.make_async_copy(lam_hbm, lam_s, lam_sem)

    barrier = pltpu.get_barrier_semaphore()
    for b in range(bits):
        pl.semaphore_signal(
            barrier, inc=1, device_id={"seq": me_seq ^ partner_mask(b)}, device_id_type=MESH
        )
    for k in range(1, head_n):
        pl.semaphore_signal(
            barrier, inc=1, device_id={"head": lax.rem(me_head + k, head_n)}, device_id_type=MESH
        )

    for h in range(heads):
        load(2, h).start()
        load(1, h).start()
    lam_copy.start()

    def state_copy(b, h):
        return pltpu.make_async_remote_copy(
            src_ref=send_s.at[b, h],
            dst_ref=recv_s.at[h, b],
            send_sem=send_sem.at[b, h],
            recv_sem=recv_sem.at[b, h],
            device_id={"seq": me_seq ^ partner_mask(b)},
            device_id_type=MESH,
        )

    for h in range(heads):
        row = jnp.broadcast_to(gain_ref[h : h + 1, :], (E, E))
        gcol_s[h] = row.T

    def states(h):
        load(2, h).wait()
        load(1, h).wait()
        load(0, h).start()
        parts = []
        for c in range(chunks):
            rows = pl.ds(c * C, C)
            vt = v_s[h, rows, :].T
            vt_s[h, :, pl.ds(c * C, C)] = vt
            parts.append(nn(vt, k_s[h, rows, :]))
        size = 1
        bit = 0
        while size < chunks:
            for start in range(0, chunks, 2 * size):
                lv_s[h, table[(bit, start)]] = parts[start // size].astype(BF16)
            parts = [parts[2 * i] + parts[2 * i + 1] for i in range(len(parts) // 2)]
            size *= 2
            bit += 1
        total = parts[0].astype(BF16)
        send_s[0, h] = total
        p_s[h] = total.astype(F32)

    states(0)
    pl.semaphore_wait(barrier, bits + head_n - 1)
    state_copy(0, 0).start()

    @pl.loop(1, heads)
    def _(h):
        states(h)
        state_copy(0, h).start()

    lam_copy.wait()
    for h in range(heads):
        lam_s[h] = lam_s[h] * scaling

    lane = lax.broadcasted_iota(jnp.int32, (8, HALF), 1)
    sub = lax.broadcasted_iota(jnp.int32, (8, HALF), 0)
    low = lane & 7
    low_x = low ^ sub
    low_ok = sub <= low
    high = lane >> 3

    def factors(h, start):
        def row(level):
            return lam_s[h, pl.ds(level, 1), pl.ds(start, HALF)]

        def wide(level):
            return jnp.broadcast_to(row(level), (8, HALF))

        fine = jnp.where(low_x < 2, wide(1), jnp.where(low_x < 4, wide(2), wide(3)))
        fine = jnp.where(low_x == 0, wide(0), fine)
        fine = jnp.where(low_ok, fine, 0.0)
        l4, l5, l6, l7 = wide(4), wide(5), wide(6), wide(7)
        pieces = []
        for half in range(2):
            a = sub + 8 * half
            x = a ^ high
            coarse = jnp.where(x < 2, l4, jnp.where(x < 4, l5, jnp.where(x < 8, l6, l7)))
            coarse = jnp.where(a < high, coarse, 0.0)
            for r in range(8):
                spread = jnp.broadcast_to(coarse[r : r + 1, :], (8, HALF))
                pieces.append(jnp.where(high == 8 * half + r, fine, spread))
        return jnp.concatenate(pieces, axis=0)

    def inside(h):
        load(0, h).wait()
        for c in range(chunks):
            rows = pl.ds(c * C, C)
            q = q_s[h, rows, :]
            lhs = [k_s[h, rows, :]]
            levels = []
            for bit in range(chunks.bit_length() - 1):
                if c >> bit & 1:
                    start = (c >> bit ^ 1) << bit
                    lhs.append(lv_s[h, table[(bit, start)]])
                    levels.append(9 + bit)
            prod = nt(jnp.concatenate(lhs, axis=0), q)
            f0 = factors(h, c * C)
            f1 = factors(h, c * C + HALF)
            l8 = lam_s[h, pl.ds(8, 1), pl.ds(c * C + HALF, HALF)]
            top = jnp.concatenate(
                [(prod[:HALF, :HALF] * f0).astype(BF16), (prod[:HALF, HALF:] * l8).astype(BF16)],
                axis=1,
            )
            bottom = jnp.concatenate(
                [jnp.zeros((HALF, HALF), BF16), (prod[HALF:C, HALF:] * f1).astype(BF16)], axis=1
            )
            weighted = jnp.concatenate([top, bottom], axis=0)
            acc = nn(vt_s[h, :, rows], weighted)
            for i, level in enumerate(levels):
                weight = lam_s[h, pl.ds(level, 1), rows]
                acc = acc + prod[C + i * E : C + (i + 1) * E] * weight
            acc_s[h, :, rows] = acc

    def relay(b, h):
        copy = state_copy(b, h)
        copy.wait_recv()
        if b + 1 < bits:
            total = p_s[h] + recv_s[h, b].astype(F32)
            p_s[h] = total
            send_s[b + 1, h] = total.astype(BF16)
            state_copy(b + 1, h).start()

    LAG = 2

    def relays(slot):
        for b in range(bits):
            h = slot - b * LAG

            @pl.when(jnp.logical_and(h >= 0, h < heads))
            def _():
                relay(b, h)

    sq_s[...] = jnp.zeros_like(sq_s)

    @pl.loop(0, heads)
    def _(h):
        relays(h)
        inside(h)

    on = [(lax.shift_right_logical(me_seq, b) & 1).astype(F32) for b in range(bits)]

    def across(h):
        pieces = 2
        step = E // pieces
        for c in range(chunks):
            rows = pl.ds(c * C, C)
            q = q_s[h, rows, :]
            weights = [lam_s[h, pl.ds(local_bits + 1 + b, 1), rows] * on[b] for b in range(bits)]
            square = sq_s[:, rows]
            lhs = [
                recv_s[h, b, pl.ds(p * step, step), :] for p in range(pieces) for b in range(bits)
            ]
            prod = nt(jnp.concatenate(lhs, axis=0), q)
            for p in range(pieces):
                acc = acc_s[h, pl.ds(p * step, step), rows]
                for b in range(bits):
                    at = (p * bits + b) * step
                    acc = acc + prod[at : at + step] * weights[b]
                acc_s[h, pl.ds(p * step, step), rows] = acc
                sq = acc * acc
                for r in range(step // 8):
                    square = square + sq[r * 8 : (r + 1) * 8]
            sq_s[:, rows] = square

    @pl.loop(0, heads)
    def _(h):
        slot = h + heads
        relays(slot)

        @pl.when(h >= (bits - 1) * LAG)
        def _():
            across(h - (bits - 1) * LAG)

    first = heads - (bits - 1) * LAG

    @pl.loop(max(first, 0), heads)
    def _(h):
        relays(h + heads + (bits - 1) * LAG)
        across(h)

    sqx_s[me_head] = jnp.sum(sq_s[...], axis=0, keepdims=True)

    def sq_copy(k):
        return pltpu.make_async_remote_copy(
            src_ref=sqx_s.at[me_head],
            dst_ref=sqx_s.at[me_head],
            send_sem=sq_send_sem.at[k],
            recv_sem=sq_recv_sem.at[k],
            device_id={"head": lax.rem(me_head + k, head_n)},
            device_id_type=MESH,
        )

    def sq_arrive(k):
        owner = lax.rem(me_head + head_n - k, head_n)
        return pltpu.make_async_remote_copy(
            src_ref=sqx_s.at[owner],
            dst_ref=sqx_s.at[owner],
            send_sem=sq_send_sem.at[k],
            recv_sem=sq_recv_sem.at[k],
            device_id={"head": lax.rem(me_head + k, head_n)},
            device_id_type=MESH,
        )

    for k in range(1, head_n):
        sq_copy(k).start()
    for k in range(1, head_n):
        sq_arrive(k).wait_recv()
    total = sqx_s[0]
    for k in range(1, head_n):
        total = total + sqx_s[k]
    scale = lax.rsqrt(total / (HEADS * E) + 1e-05)
    sqx_s[head_n] = scale

    @pl.loop(0, heads)
    def _(h):
        cols = pl.ds(pl.multiple_of(h * E, E), E)
        for c in range(tokens // HALF):
            rows = pl.ds(c * HALF, HALF)
            value = acc_s[h, :, rows] * gcol_s[h] * sqx_s[head_n, :, rows]
            out_ref[rows, cols] = value.astype(BF16).T

    for b in range(bits):
        for h in range(heads):
            state_copy(b, h).wait_send()
    for k in range(1, head_n):
        sq_copy(k).wait_send()


def body(queries, key_vectors, value_vectors, level_weights, norm_gain):
    tokens = queries.shape[0]
    heads, levels = level_weights.shape[:2]
    seq_n = lax.axis_size("seq")
    head_n = lax.axis_size("head")
    bits = seq_n.bit_length() - 1
    slots = max(len(buckets_of(tokens // C)), 1)
    any_spec = pl.BlockSpec(memory_space=pl.ANY)
    vmem = pl.BlockSpec(memory_space=pltpu.VMEM)
    return pl.pallas_call(
        functools.partial(kernel, seq_n, head_n, heads, tokens),
        out_shape=jax.ShapeDtypeStruct((tokens, heads * E), BF16),
        in_specs=[any_spec] * 4 + [vmem],
        out_specs=vmem,
        scratch_shapes=[
            pltpu.VMEM((heads, tokens, D), BF16),
            pltpu.VMEM((heads, tokens, D), BF16),
            pltpu.VMEM((heads, tokens, E), BF16),
            pltpu.VMEM((heads, levels, tokens), F32),
            pltpu.VMEM((heads, E, tokens), BF16),
            pltpu.VMEM((heads, E, tokens), F32),
            pltpu.VMEM((heads, slots, E, D), BF16),
            pltpu.VMEM((heads, E, D), F32),
            pltpu.VMEM((bits, heads, E, D), BF16),
            pltpu.VMEM((heads, bits, E, D), BF16),
            pltpu.VMEM((8, tokens), F32),
            pltpu.VMEM((head_n + 1, 1, tokens), F32),
            pltpu.VMEM((heads, E, E), F32),
            pltpu.VMEM((8, HALF), F32),
            pltpu.VMEM((16, HALF), F32),
            pltpu.SemaphoreType.DMA((3, heads)),
            pltpu.SemaphoreType.DMA,
            pltpu.SemaphoreType.DMA((bits, heads)),
            pltpu.SemaphoreType.DMA((bits, heads)),
            pltpu.SemaphoreType.DMA((head_n,)),
            pltpu.SemaphoreType.DMA((head_n,)),
        ],
        compiler_params=pltpu.CompilerParams(
            collective_id=0, has_side_effects=True, vmem_limit_bytes=60 * 1024 * 1024
        ),
        name="fenwick",
    )(queries, key_vectors, value_vectors, level_weights, norm_gain.reshape(heads, E))


def solution(mesh):
    placed = (
        P("seq", "head"),
        P("seq", "head"),
        P("seq", "head"),
        P("head", None, "seq"),
        P("head"),
    )
    return jax.shard_map(
        body, mesh=mesh, in_specs=placed, out_specs=P("seq", "head"), check_vma=False
    )
```

```python
import functools

import jax
import jax.numpy as jnp
from jax import lax
from jax.experimental import pallas as pl
from jax.experimental.pallas import tpu as pltpu
from jax.sharding import PartitionSpec as P

D = 128
E = 128
C = 256
HALF = 128
HEADS = 64
LAG = 5
RATE = 4
AHEAD = 3
MESH = pl.DeviceIdType.MESH
F32 = jnp.float32
BF16 = jnp.bfloat16


def nt(a, b):
    return lax.dot_general(a, b, (((1,), (1,)), ((), ())), preferred_element_type=F32)


def nn(a, b):
    return lax.dot_general(a, b, (((1,), (0,)), ((), ())), preferred_element_type=F32)


def partner_mask(bit):
    return 1 << bit if bit % 2 == 0 else 3 << (bit - 1)


def buckets_of(chunks):
    table = {}
    bit = 0
    while 1 << bit < chunks:
        for start in range(0, chunks, 2 << bit):
            table[(bit, start)] = len(table)
        bit += 1
    return table


def kernel(
    seq_n, head_n, heads, tokens,
    q_hbm, k_hbm, v_hbm, lam_hbm, gain_ref,
    out_ref, scale_ref,
    q_s, k_s, v_s, lam_s, vt_s, acc_s, lv_s, p_s, send_s, recv_s, sq_s, sqx_s, w_s, qt_s, x_s,
    load_sem, lam_sem, send_sem, recv_sem, sq_send_sem, sq_recv_sem,
):
    chunks = tokens // C
    bits = seq_n.bit_length() - 1
    local_bits = tokens.bit_length() - 1
    me_seq = lax.axis_index("seq")
    me_head = lax.axis_index("head")
    table = buckets_of(chunks)
    scaling = D ** (-0.5)

    def load(which, h):
        src, dst = ((q_hbm, q_s), (k_hbm, k_s), (v_hbm, v_s))[which]
        cols = pl.ds(pl.multiple_of(h * D, D), D)
        return pltpu.make_async_copy(src.at[:, cols], dst.at[h], load_sem.at[which, h])

    lam_copy = pltpu.make_async_copy(lam_hbm, lam_s, lam_sem)

    for h in range(AHEAD):
        load(2, h).start()
        load(1, h).start()

    barrier = pltpu.get_barrier_semaphore()
    for b in range(bits):
        pl.semaphore_signal(
            barrier, inc=1, device_id={"seq": me_seq ^ partner_mask(b)}, device_id_type=MESH
        )
    for k in range(1, head_n):
        pl.semaphore_signal(
            barrier, inc=1, device_id={"head": lax.rem(me_head + k, head_n)}, device_id_type=MESH
        )

    def state_copy(b, h):
        return pltpu.make_async_remote_copy(
            src_ref=send_s.at[b, h],
            dst_ref=recv_s.at[h, b],
            send_sem=send_sem.at[b, h],
            recv_sem=recv_sem.at[b, h],
            device_id={"seq": me_seq ^ partner_mask(b)},
            device_id_type=MESH,
        )

    def states(h):
        load(2, h).wait()
        load(1, h).wait()
        parts = []
        for c in range(chunks):
            rows = pl.ds(c * C, C)
            vt = v_s[h, rows, :].T
            vt_s[h, :, pl.ds(c * C, C)] = vt
            parts.append(nn(vt, k_s[h, rows, :]))
        size = 1
        bit = 0
        while size < chunks:
            for start in range(0, chunks, 2 * size):
                lv_s[h, table[(bit, start)]] = parts[start // size].astype(BF16)
            parts = [parts[2 * i] + parts[2 * i + 1] for i in range(len(parts) // 2)]
            size *= 2
            bit += 1
        total = parts[0].astype(BF16)
        send_s[0, h] = total
        p_s[h] = total.astype(F32)

    states(0)
    load(2, AHEAD).start()
    load(1, AHEAD).start()
    pl.semaphore_wait(barrier, bits + head_n - 1)
    state_copy(0, 0).start()

    @pl.loop(1, heads)
    def _(h):
        states(h)
        state_copy(0, h).start()

        @pl.when(h + AHEAD < heads)
        def _():
            load(2, h + AHEAD).start()
            load(1, h + AHEAD).start()

        @pl.when(h + AHEAD == heads)
        def _():
            load(0, 0).start()
            lam_copy.start()

        @pl.when(h + AHEAD > heads)
        def _():
            load(0, h + AHEAD - heads).start()

    for h in range(AHEAD, heads):
        load(0, h).start()
    for c in range(chunks):
        w_s[c, HALF:C, :HALF] = jnp.zeros((HALF, HALF), BF16)
    lam_copy.wait()
    for h in range(heads):
        lam_s[h] = lam_s[h] * scaling

    lane = lax.broadcasted_iota(jnp.int32, (8, HALF), 1)
    sub = lax.broadcasted_iota(jnp.int32, (8, HALF), 0)
    low = lane & 7
    low_x = low ^ sub
    low_ok = sub <= low
    high = lane >> 3

    def factors(h, start):
        def row(level):
            return lam_s[h, pl.ds(level, 1), pl.ds(start, HALF)]

        def wide(level):
            return jnp.broadcast_to(row(level), (8, HALF))

        fine = jnp.where(low_x < 2, wide(1), jnp.where(low_x < 4, wide(2), wide(3)))
        fine = jnp.where(low_x == 0, wide(0), fine)
        fine = jnp.where(low_ok, fine, 0.0)
        l4, l5, l6, l7 = wide(4), wide(5), wide(6), wide(7)
        pieces = []
        for half in range(2):
            a = sub + 8 * half
            x = a ^ high
            coarse = jnp.where(x < 2, l4, jnp.where(x < 4, l5, jnp.where(x < 8, l6, l7)))
            coarse = jnp.where(a < high, coarse, 0.0)
            for r in range(8):
                spread = jnp.broadcast_to(coarse[r : r + 1, :], (8, HALF))
                pieces.append(jnp.where(high == 8 * half + r, fine, spread))
        return jnp.concatenate(pieces, axis=0)

    def levels_of(c):
        found = []
        for bit in range(chunks.bit_length() - 1):
            if c >> bit & 1:
                found.append((9 + bit, table[(bit, (c >> bit ^ 1) << bit)]))
        return found

    def turn(h, c):
        rows = pl.ds(c * C, C)
        qt = q_s[h, rows, :].T
        qt_s[h, :, rows] = qt
        wide = qt.astype(F32)
        for i, (level, _) in enumerate(levels_of(c)):
            scaled = (wide * lam_s[h, pl.ds(level, 1), rows]).astype(BF16)
            w_s[c, pl.ds(C + i * D, D), :] = scaled

    def score(h, c):
        rows = pl.ds(c * C, C)
        prod = nn(k_s[h, rows, :], qt_s[h, :, rows])
        f0 = factors(h, c * C)
        l8 = lam_s[h, pl.ds(8, 1), pl.ds(c * C + HALF, HALF)]
        at = c
        w_s[at, :HALF, :HALF] = (prod[:HALF, :HALF] * f0).astype(BF16)
        w_s[at, :HALF, HALF:] = (prod[:HALF, HALF:] * l8).astype(BF16)
        f1 = factors(h, c * C + HALF)
        w_s[at, HALF:C, HALF:] = (prod[HALF:, HALF:] * f1).astype(BF16)

    def gather(h, c):
        rows = pl.ds(c * C, C)
        lhs = [vt_s[h, :, rows]] + [lv_s[h, slot] for _, slot in levels_of(c)]
        depth = C + D * (len(lhs) - 1)
        acc_s[h, :, rows] = nn(jnp.concatenate(lhs, axis=1), w_s[c, :depth, :])

    def relay(b, h):
        copy = state_copy(b, h)
        copy.wait_recv()
        if b + 1 < bits:
            total = p_s[h] + recv_s[h, b].astype(F32)
            p_s[h] = total
            send_s[b + 1, h] = total.astype(BF16)
            state_copy(b + 1, h).start()

    def tick(u):
        for b in range(bits):
            h = u - b * LAG

            @pl.when(jnp.logical_and(h >= 0, h < heads))
            def _():
                relay(b, h)

    def due(step):
        return step * RATE // 3

    sq_s[...] = jnp.zeros_like(sq_s)

    @pl.loop(0, heads)
    def _(h):
        pl.loop(due(jnp.maximum(h - 1, 0)), due(h))(tick)
        load(0, h).wait()
        for c in range(chunks):
            turn(h, c)
        for c in range(chunks):
            score(h, c)
        for c in range(chunks):
            gather(h, c)

    on = [(lax.shift_right_logical(me_seq, b) & 1).astype(F32) for b in range(bits)]

    def across(h):
        cols = pl.ds(pl.multiple_of(h * E, E), E)
        def spread(c):
            rows = pl.ds(c * C, C)
            wide = qt_s[h, :, rows].astype(F32)
            for b in range(bits):
                weight = lam_s[h, pl.ds(local_bits + 1 + b, 1), rows] * on[b]
                x_s[c, pl.ds(b * D, D), :] = (wide * weight).astype(BF16)

        def read(c):
            rows = pl.ds(c * C, C)
            lhs = jnp.concatenate([recv_s[h, b] for b in range(bits)], axis=1)
            acc = acc_s[h, :, rows] + nn(lhs, x_s[c])
            out_ref[rows, cols] = acc.T * gain_ref[pl.ds(h, 1), :]
            sq = acc * acc
            square = sq_s[:, rows]
            for r in range(E // 8):
                square = square + sq[r * 8 : (r + 1) * 8]
            sq_s[:, rows] = square

        for c in range(chunks):
            spread(c)
        for c in range(chunks):
            read(c)

    last = (bits - 1) * LAG

    @pl.loop(min(due(heads - 1), last), heads + last)
    def _(u):
        @pl.when(u >= due(heads - 1))
        def _():
            tick(u)

        @pl.when(u >= last)
        def _():
            across(u - last)

    sqx_s[me_head] = jnp.sum(sq_s[...], axis=0, keepdims=True)

    def sq_copy(k):
        return pltpu.make_async_remote_copy(
            src_ref=sqx_s.at[me_head],
            dst_ref=sqx_s.at[me_head],
            send_sem=sq_send_sem.at[k],
            recv_sem=sq_recv_sem.at[k],
            device_id={"head": lax.rem(me_head + k, head_n)},
            device_id_type=MESH,
        )

    def sq_arrive(k):
        owner = lax.rem(me_head + head_n - k, head_n)
        return pltpu.make_async_remote_copy(
            src_ref=sqx_s.at[owner],
            dst_ref=sqx_s.at[owner],
            send_sem=sq_send_sem.at[k],
            recv_sem=sq_recv_sem.at[k],
            device_id={"head": lax.rem(me_head + k, head_n)},
            device_id_type=MESH,
        )

    for k in range(1, head_n):
        sq_copy(k).start()

    @pl.loop(0, heads)
    def _(h):
        for b in range(bits):
            state_copy(b, h).wait_send()

    for k in range(1, head_n):
        sq_arrive(k).wait_recv()
    total = sqx_s[0]
    for k in range(1, head_n):
        total = total + sqx_s[k]
    scale_ref[...] = lax.rsqrt(total / (HEADS * E) + 1e-05)

    for k in range(1, head_n):
        sq_copy(k).wait_send()


def finish(tokens, acc_ref, scale_ref, out_hbm, buf, col_s, sem):
    def out_copy(i):
        rows = pl.ds(i * HALF, HALF)
        return pltpu.make_async_copy(buf.at[i], out_hbm.at[rows, :], sem.at[i])

    def turn(i):
        rows = pl.ds(i * HALF, HALF)
        col_s[rows, :] = jnp.broadcast_to(scale_ref[:, rows], (HALF, HALF)).T

    blocks = tokens // HALF
    turn(0)
    for i in range(blocks):
        if i + 1 < blocks:
            turn(i + 1)
        rows = pl.ds(i * HALF, HALF)
        for h in range(acc_ref.shape[1] // E):
            cols = pl.ds(h * E, E)
            buf[i, :, cols] = (acc_ref[rows, cols] * col_s[rows, :]).astype(BF16)
        out_copy(i).start()
    for i in range(blocks):
        out_copy(i).wait()


def body(queries, key_vectors, value_vectors, level_weights, norm_gain):
    tokens = queries.shape[0]
    heads, levels = level_weights.shape[:2]
    seq_n = lax.axis_size("seq")
    head_n = lax.axis_size("head")
    bits = seq_n.bit_length() - 1
    slots = max(len(buckets_of(tokens // C)), 1)
    any_spec = pl.BlockSpec(memory_space=pl.ANY)
    vmem = pl.BlockSpec(memory_space=pltpu.VMEM)
    mixture, scale = pl.pallas_call(
        functools.partial(kernel, seq_n, head_n, heads, tokens),
        out_shape=(pltpu.VMEM((tokens, heads * E), F32), pltpu.VMEM((1, tokens), F32)),
        in_specs=[pl.BlockSpec(memory_space=pltpu.HBM)] * 4 + [vmem],
        out_specs=(vmem, vmem),
        scratch_shapes=[
            pltpu.VMEM((heads, tokens, D), BF16),
            pltpu.VMEM((heads, tokens, D), BF16),
            pltpu.VMEM((heads, tokens, E), BF16),
            pltpu.VMEM((heads, levels, tokens), F32),
            pltpu.VMEM((heads, E, tokens), BF16),
            pltpu.VMEM((heads, E, tokens), F32),
            pltpu.VMEM((heads, slots, E, D), BF16),
            pltpu.VMEM((heads, E, D), F32),
            pltpu.VMEM((bits, heads, E, D), BF16),
            pltpu.VMEM((heads, bits, E, D), BF16),
            pltpu.VMEM((8, tokens), F32),
            pltpu.VMEM((head_n, 1, tokens), F32),
            pltpu.VMEM((tokens // C, C + 3 * D, C), BF16),
            pltpu.VMEM((heads, D, tokens), BF16),
            pltpu.VMEM((tokens // C, bits * D, C), BF16),
            pltpu.SemaphoreType.DMA((3, heads)),
            pltpu.SemaphoreType.DMA,
            pltpu.SemaphoreType.DMA((bits, heads)),
            pltpu.SemaphoreType.DMA((bits, heads)),
            pltpu.SemaphoreType.DMA((head_n,)),
            pltpu.SemaphoreType.DMA((head_n,)),
        ],
        compiler_params=pltpu.CompilerParams(
            collective_id=0, has_side_effects=True, vmem_limit_bytes=58 * 1000 * 1000
        ),
        name="fenwick",
    )(queries, key_vectors, value_vectors, level_weights, norm_gain.reshape(heads, E))
    return pl.pallas_call(
        functools.partial(finish, tokens),
        out_shape=jax.ShapeDtypeStruct((tokens, heads * E), BF16),
        in_specs=[vmem, vmem],
        out_specs=any_spec,
        scratch_shapes=[
            pltpu.VMEM((tokens // HALF, HALF, heads * E), BF16),
            pltpu.VMEM((tokens, HALF), F32),
            pltpu.SemaphoreType.DMA((tokens // HALF,)),
        ],
        compiler_params=pltpu.CompilerParams(vmem_limit_bytes=16 * 1024 * 1024),
        name="finish",
    )(mixture, scale)


def solution(mesh):
    placed = (
        P("seq", "head"),
        P("seq", "head"),
        P("seq", "head"),
        P("head", None, "seq"),
        P("head"),
    )
    return jax.shard_map(
        body, mesh=mesh, in_specs=placed, out_specs=P("seq", "head"), check_vma=False
    )
```

```python
import functools

import jax
import jax.numpy as jnp
from jax import lax
from jax.experimental import pallas as pl
from jax.experimental.pallas import tpu as pltpu
from jax.sharding import PartitionSpec as P

D = 128
E = 128
C = 256
HALF = 128
HEADS = 64
LAG = 4
RATE = 4
AHEAD = 3
MESH = pl.DeviceIdType.MESH
F32 = jnp.float32
BF16 = jnp.bfloat16


def nt(a, b):
    return lax.dot_general(a, b, (((1,), (1,)), ((), ())), preferred_element_type=F32)


def nn(a, b):
    return lax.dot_general(a, b, (((1,), (0,)), ((), ())), preferred_element_type=F32)


def partner_mask(bit):
    return 1 << bit if bit % 2 == 0 else 3 << (bit - 1)


def scaled(qt, row):
    width = qt.shape[1]
    weight = jnp.broadcast_to(row, (16, width)).astype(BF16)
    return qt * jnp.concatenate([weight] * (qt.shape[0] // 16), axis=0)


def buckets_of(chunks):
    table = {}
    bit = 0
    while 1 << bit < chunks:
        for start in range(0, chunks, 2 << bit):
            table[(bit, start)] = len(table)
        bit += 1
    return table


def kernel(
    seq_n, head_n, heads, tokens,
    q_hbm, k_hbm, v_hbm, lam_hbm, gain_ref,
    out_ref, scale_ref,
    q_s, k_s, v_s, lam_s, vt_s, acc_s, lv_s, p_s, send_s, recv_s, sq_s, sqx_s, w_s, qt_s, x_s,
    load_sem, lam_sem, send_sem, recv_sem, sq_send_sem, sq_recv_sem,
):
    chunks = tokens // C
    bits = seq_n.bit_length() - 1
    local_bits = tokens.bit_length() - 1
    me_seq = lax.axis_index("seq")
    me_head = lax.axis_index("head")
    table = buckets_of(chunks)
    scaling = D ** (-0.5)

    def load(which, h):
        src, dst = ((q_hbm, q_s), (k_hbm, k_s), (v_hbm, v_s))[which]
        cols = pl.ds(pl.multiple_of(h * D, D), D)
        return pltpu.make_async_copy(src.at[:, cols], dst.at[h], load_sem.at[which, h])

    lam_copy = pltpu.make_async_copy(lam_hbm, lam_s, lam_sem)

    for h in range(AHEAD):
        load(2, h).start()
        load(1, h).start()

    barrier = pltpu.get_barrier_semaphore()
    for b in range(bits):
        pl.semaphore_signal(
            barrier, inc=1, device_id={"seq": me_seq ^ partner_mask(b)}, device_id_type=MESH
        )
    for k in range(1, head_n):
        pl.semaphore_signal(
            barrier, inc=1, device_id={"head": lax.rem(me_head + k, head_n)}, device_id_type=MESH
        )

    def state_copy(b, h):
        return pltpu.make_async_remote_copy(
            src_ref=send_s.at[b, h],
            dst_ref=recv_s.at[h, b],
            send_sem=send_sem.at[b, h],
            recv_sem=recv_sem.at[b, h],
            device_id={"seq": me_seq ^ partner_mask(b)},
            device_id_type=MESH,
        )

    sends = [me_seq < seq_n - (1 << b) for b in range(bits)]
    gets = [(me_seq ^ partner_mask(b)) < seq_n - (1 << b) for b in range(bits)]

    def send_state(b, h):
        @pl.when(sends[b])
        def _():
            state_copy(b, h).start()

    def states(h):
        load(2, h).wait()
        load(1, h).wait()
        parts = []
        for c in range(chunks):
            rows = pl.ds(c * C, C)
            vt = v_s[h, rows, :].T
            vt_s[h, :, pl.ds(c * C, C)] = vt
            parts.append(nn(vt, k_s[h, rows, :]))
        size = 1
        bit = 0
        while size < chunks:
            for start in range(0, chunks, 2 * size):
                lv_s[h, table[(bit, start)]] = parts[start // size].astype(BF16)
            parts = [parts[2 * i] + parts[2 * i + 1] for i in range(len(parts) // 2)]
            size *= 2
            bit += 1
        total = parts[0].astype(BF16)
        send_s[0, h] = total
        p_s[h] = total.astype(F32)

    states(0)
    load(2, AHEAD).start()
    load(1, AHEAD).start()
    pl.semaphore_wait(barrier, bits + head_n - 1)
    send_state(0, 0)

    @pl.loop(1, heads)
    def _(h):
        states(h)
        send_state(0, h)

        @pl.when(h + AHEAD < heads)
        def _():
            load(2, h + AHEAD).start()
            load(1, h + AHEAD).start()

        @pl.when(h + AHEAD == heads)
        def _():
            load(0, 0).start()
            lam_copy.start()

        @pl.when(h + AHEAD > heads)
        def _():
            load(0, h + AHEAD - heads).start()

    for h in range(AHEAD, heads):
        load(0, h).start()
    for c in range(chunks):
        w_s[c, HALF:C, :HALF] = jnp.zeros((HALF, HALF), BF16)
    lam_copy.wait()
    for h in range(heads):
        lam_s[h] = lam_s[h] * scaling

    lane = lax.broadcasted_iota(jnp.int32, (8, HALF), 1)
    sub = lax.broadcasted_iota(jnp.int32, (8, HALF), 0)
    low = lane & 7
    low_x = low ^ sub
    low_ok = sub <= low
    high = lane >> 3

    def factors(h, start):
        def row(level):
            return lam_s[h, pl.ds(level, 1), pl.ds(start, HALF)]

        def wide(level):
            return jnp.broadcast_to(row(level), (8, HALF))

        fine = jnp.where(low_x < 2, wide(1), jnp.where(low_x < 4, wide(2), wide(3)))
        fine = jnp.where(low_x == 0, wide(0), fine)
        fine = jnp.where(low_ok, fine, 0.0)
        l4, l5, l6, l7 = wide(4), wide(5), wide(6), wide(7)
        pieces = []
        for half in range(2):
            a = sub + 8 * half
            x = a ^ high
            coarse = jnp.where(x < 2, l4, jnp.where(x < 4, l5, jnp.where(x < 8, l6, l7)))
            coarse = jnp.where(a < high, coarse, 0.0)
            for r in range(8):
                spread = jnp.broadcast_to(coarse[r : r + 1, :], (8, HALF))
                pieces.append(jnp.where(high == 8 * half + r, fine, spread))
        return jnp.concatenate(pieces, axis=0)

    def levels_of(c):
        found = []
        for bit in range(chunks.bit_length() - 1):
            if c >> bit & 1:
                found.append((9 + bit, table[(bit, (c >> bit ^ 1) << bit)]))
        return found

    def turn(h, c):
        rows = pl.ds(c * C, C)
        qt = q_s[h, rows, :].T
        qt_s[h, :, rows] = qt
        for i, (level, _) in enumerate(levels_of(c)):
            w_s[c, pl.ds(C + i * D, D), :] = scaled(qt, lam_s[h, pl.ds(level, 1), rows])

    def score(h, c):
        rows = pl.ds(c * C, C)
        prod = nn(k_s[h, rows, :], qt_s[h, :, rows])
        f0 = factors(h, c * C)
        l8 = lam_s[h, pl.ds(8, 1), pl.ds(c * C + HALF, HALF)]
        at = c
        w_s[at, :HALF, :HALF] = (prod[:HALF, :HALF] * f0).astype(BF16)
        w_s[at, :HALF, HALF:] = (prod[:HALF, HALF:] * l8).astype(BF16)
        f1 = factors(h, c * C + HALF)
        w_s[at, HALF:C, HALF:] = (prod[HALF:, HALF:] * f1).astype(BF16)

    def gather(h, c):
        rows = pl.ds(c * C, C)
        lhs = [vt_s[h, :, rows]] + [lv_s[h, slot] for _, slot in levels_of(c)]
        depth = C + D * (len(lhs) - 1)
        acc_s[h, :, rows] = nn(jnp.concatenate(lhs, axis=1), w_s[c, :depth, :])

    def relay(b, h):
        @pl.when(gets[b])
        def _():
            state_copy(b, h).wait_recv()
            if b + 1 < bits:
                @pl.when(sends[b + 1])
                def _():
                    total = p_s[h] + recv_s[h, b].astype(F32)
                    p_s[h] = total
                    send_s[b + 1, h] = total.astype(BF16)
                    state_copy(b + 1, h).start()

    def tick(u):
        for b in range(bits):
            h = u - b * LAG

            @pl.when(jnp.logical_and(h >= 0, h < heads))
            def _():
                relay(b, h)

    def due(step):
        return step * RATE // 3

    sq_s[...] = jnp.zeros_like(sq_s)
    for b in range(bits):
        @pl.when(jnp.logical_not(gets[b]))
        def _():
            for h in range(heads):
                recv_s[h, b] = jnp.zeros((E, D), BF16)


    @pl.loop(0, heads)
    def _(h):
        pl.loop(due(jnp.maximum(h - 1, 0)), due(h))(tick)
        load(0, h).wait()
        for c in range(chunks):
            turn(h, c)
        for c in range(chunks):
            score(h, c)
        for c in range(chunks):
            gather(h, c)

    on = [(lax.shift_right_logical(me_seq, b) & 1).astype(F32) for b in range(bits)]

    def across(h):
        cols = pl.ds(pl.multiple_of(h * E, E), E)
        def spread(c):
            rows = pl.ds(c * C, C)
            qt = qt_s[h, :, rows]
            for b in range(bits):
                weight = lam_s[h, pl.ds(local_bits + 1 + b, 1), rows] * on[b]
                x_s[c, pl.ds(b * D, D), :] = scaled(qt, weight)

        def read(c):
            rows = pl.ds(c * C, C)
            lhs = jnp.concatenate([recv_s[h, b] for b in range(bits)], axis=1)
            acc = acc_s[h, :, rows] + nn(lhs, x_s[c])
            out_ref[rows, cols] = acc.T * gain_ref[pl.ds(h, 1), :]
            sq = acc * acc
            square = sq_s[:, rows]
            for r in range(E // 8):
                square = square + sq[r * 8 : (r + 1) * 8]
            sq_s[:, rows] = square

        for c in range(chunks):
            spread(c)
        for c in range(chunks):
            read(c)

    last = (bits - 1) * LAG

    @pl.loop(min(due(heads - 1), last), heads + last)
    def _(u):
        @pl.when(u >= due(heads - 1))
        def _():
            tick(u)

        @pl.when(u >= last)
        def _():
            across(u - last)

    sqx_s[me_head] = jnp.sum(sq_s[...], axis=0, keepdims=True)

    def sq_copy(k):
        return pltpu.make_async_remote_copy(
            src_ref=sqx_s.at[me_head],
            dst_ref=sqx_s.at[me_head],
            send_sem=sq_send_sem.at[k],
            recv_sem=sq_recv_sem.at[k],
            device_id={"head": lax.rem(me_head + k, head_n)},
            device_id_type=MESH,
        )

    def sq_arrive(k):
        owner = lax.rem(me_head + head_n - k, head_n)
        return pltpu.make_async_remote_copy(
            src_ref=sqx_s.at[owner],
            dst_ref=sqx_s.at[owner],
            send_sem=sq_send_sem.at[k],
            recv_sem=sq_recv_sem.at[k],
            device_id={"head": lax.rem(me_head + k, head_n)},
            device_id_type=MESH,
        )

    for k in sorted(range(1, head_n), key=lambda k: abs(k - head_n // 2)):
        sq_copy(k).start()

    @pl.loop(0, heads)
    def _(h):
        for b in range(bits):
            @pl.when(sends[b])
            def _():
                state_copy(b, h).wait_send()

    for k in range(1, head_n):
        sq_arrive(k).wait_recv()
    total = sqx_s[0]
    for k in range(1, head_n):
        total = total + sqx_s[k]
    scale_ref[...] = lax.rsqrt(total / (HEADS * E) + 1e-05)

    for k in range(1, head_n):
        sq_copy(k).wait_send()


def finish(tokens, acc_ref, scale_ref, out_hbm, buf, col_s, sem):
    def out_copy(i):
        rows = pl.ds(i * HALF, HALF)
        return pltpu.make_async_copy(buf.at[i], out_hbm.at[rows, :], sem.at[i])

    def turn(i):
        rows = pl.ds(i * HALF, HALF)
        col_s[rows, :] = jnp.broadcast_to(scale_ref[:, rows], (HALF, HALF)).T

    blocks = tokens // HALF
    turn(0)
    for i in range(blocks):
        if i + 1 < blocks:
            turn(i + 1)
        rows = pl.ds(i * HALF, HALF)
        for h in range(acc_ref.shape[1] // E):
            cols = pl.ds(h * E, E)
            buf[i, :, cols] = (acc_ref[rows, cols] * col_s[rows, :]).astype(BF16)
        out_copy(i).start()
    for i in range(blocks):
        out_copy(i).wait()


def body(queries, key_vectors, value_vectors, level_weights, norm_gain):
    tokens = queries.shape[0]
    heads, levels = level_weights.shape[:2]
    seq_n = lax.axis_size("seq")
    head_n = lax.axis_size("head")
    bits = seq_n.bit_length() - 1
    slots = max(len(buckets_of(tokens // C)), 1)
    any_spec = pl.BlockSpec(memory_space=pl.ANY)
    vmem = pl.BlockSpec(memory_space=pltpu.VMEM)
    mixture, scale = pl.pallas_call(
        functools.partial(kernel, seq_n, head_n, heads, tokens),
        out_shape=(pltpu.VMEM((tokens, heads * E), F32), pltpu.VMEM((1, tokens), F32)),
        in_specs=[pl.BlockSpec(memory_space=pltpu.HBM)] * 4 + [vmem],
        out_specs=(vmem, vmem),
        scratch_shapes=[
            pltpu.VMEM((heads, tokens, D), BF16),
            pltpu.VMEM((heads, tokens, D), BF16),
            pltpu.VMEM((heads, tokens, E), BF16),
            pltpu.VMEM((heads, levels, tokens), F32),
            pltpu.VMEM((heads, E, tokens), BF16),
            pltpu.VMEM((heads, E, tokens), F32),
            pltpu.VMEM((heads, slots, E, D), BF16),
            pltpu.VMEM((heads, E, D), F32),
            pltpu.VMEM((bits, heads, E, D), BF16),
            pltpu.VMEM((heads, bits, E, D), BF16),
            pltpu.VMEM((8, tokens), F32),
            pltpu.VMEM((head_n, 1, tokens), F32),
            pltpu.VMEM((tokens // C, C + 3 * D, C), BF16),
            pltpu.VMEM((heads, D, tokens), BF16),
            pltpu.VMEM((tokens // C, bits * D, C), BF16),
            pltpu.SemaphoreType.DMA((3, heads)),
            pltpu.SemaphoreType.DMA,
            pltpu.SemaphoreType.DMA((bits, heads)),
            pltpu.SemaphoreType.DMA((bits, heads)),
            pltpu.SemaphoreType.DMA((head_n,)),
            pltpu.SemaphoreType.DMA((head_n,)),
        ],
        compiler_params=pltpu.CompilerParams(
            collective_id=0, has_side_effects=True, vmem_limit_bytes=58 * 1000 * 1000
        ),
        name="fenwick",
    )(queries, key_vectors, value_vectors, level_weights, norm_gain.reshape(heads, E))
    return pl.pallas_call(
        functools.partial(finish, tokens),
        out_shape=jax.ShapeDtypeStruct((tokens, heads * E), BF16),
        in_specs=[vmem, vmem],
        out_specs=any_spec,
        scratch_shapes=[
            pltpu.VMEM((tokens // HALF, HALF, heads * E), BF16),
            pltpu.VMEM((tokens, HALF), F32),
            pltpu.SemaphoreType.DMA((tokens // HALF,)),
        ],
        compiler_params=pltpu.CompilerParams(vmem_limit_bytes=16 * 1024 * 1024),
        name="finish",
    )(mixture, scale)


def solution(mesh):
    placed = (
        P("seq", "head"),
        P("seq", "head"),
        P("seq", "head"),
        P("head", None, "seq"),
        P("head"),
    )
    return jax.shard_map(
        body, mesh=mesh, in_specs=placed, out_specs=P("seq", "head"), check_vma=False
    )
```

```python
import functools

import jax
import jax.numpy as jnp
from jax import lax
from jax.experimental import pallas as pl
from jax.experimental.pallas import tpu as pltpu
from jax.sharding import PartitionSpec as P

D = 128
E = 128
C = 256
HALF = 128
HEADS = 64
LAG = 4
RATE = 4
AHEAD = 8
MESH = pl.DeviceIdType.MESH
F32 = jnp.float32
BF16 = jnp.bfloat16


def nt(a, b):
    return lax.dot_general(a, b, (((1,), (1,)), ((), ())), preferred_element_type=F32)


def nn(a, b):
    return lax.dot_general(a, b, (((1,), (0,)), ((), ())), preferred_element_type=F32)


def partner_mask(bit):
    return 1 << bit if bit % 2 == 0 else 3 << (bit - 1)


def scaled(qt, row):
    width = qt.shape[1]
    weight = jnp.broadcast_to(row, (16, width)).astype(BF16)
    return qt * jnp.concatenate([weight] * (qt.shape[0] // 16), axis=0)


def buckets_of(chunks):
    table = {}
    bit = 0
    while 1 << bit < chunks:
        for start in range(0, chunks, 2 << bit):
            table[(bit, start)] = len(table)
        bit += 1
    return table


def kernel(
    seq_n, head_n, heads, tokens,
    q_hbm, k_hbm, v_hbm, lam_hbm, gain_ref,
    out_ref, scale_ref,
    q_s, k_s, v_s, lam_s, vt_s, acc_s, lv_s, p_s, send_s, recv_s, sq_s, sqx_s, w_s, qt_s, x_s,
    load_sem, lam_sem, send_sem, recv_sem, sq_send_sem, sq_recv_sem,
):
    chunks = tokens // C
    bits = seq_n.bit_length() - 1
    local_bits = tokens.bit_length() - 1
    me_seq = lax.axis_index("seq")
    me_head = lax.axis_index("head")
    table = buckets_of(chunks)
    scaling = D ** (-0.5)

    def load(which, h):
        src, dst = ((q_hbm, q_s), (k_hbm, k_s), (v_hbm, v_s))[which]
        cols = pl.ds(pl.multiple_of(h * D, D), D)
        return pltpu.make_async_copy(src.at[:, cols], dst.at[h], load_sem.at[which, h])

    lam_copy = pltpu.make_async_copy(lam_hbm, lam_s, lam_sem)

    barrier = pltpu.get_barrier_semaphore()
    for k in sorted(range(1, head_n), key=lambda k: abs(k - head_n // 2)):
        pl.semaphore_signal(
            barrier, inc=1, device_id={"head": lax.rem(me_head + k, head_n)}, device_id_type=MESH
        )

    for h in range(AHEAD):
        load(2, h).start()
        load(1, h).start()

    for b in range(bits):
        pl.semaphore_signal(
            barrier, inc=1, device_id={"seq": me_seq ^ partner_mask(b)}, device_id_type=MESH
        )

    def state_copy(b, h):
        return pltpu.make_async_remote_copy(
            src_ref=send_s.at[b, h],
            dst_ref=recv_s.at[h, b],
            send_sem=send_sem.at[b, h],
            recv_sem=recv_sem.at[b, h],
            device_id={"seq": me_seq ^ partner_mask(b)},
            device_id_type=MESH,
        )

    sends = [me_seq < seq_n - (1 << b) for b in range(bits)]
    gets = [(me_seq ^ partner_mask(b)) < seq_n - (1 << b) for b in range(bits)]

    def send_state(b, h):
        @pl.when(sends[b])
        def _():
            state_copy(b, h).start()

    def states(h):
        load(2, h).wait()
        load(1, h).wait()
        parts = []
        for c in range(chunks):
            rows = pl.ds(c * C, C)
            vt = v_s[h, rows, :].T
            vt_s[h, :, pl.ds(c * C, C)] = vt
            parts.append(nn(vt, k_s[h, rows, :]))
        size = 1
        bit = 0
        while size < chunks:
            for start in range(0, chunks, 2 * size):
                lv_s[h, table[(bit, start)]] = parts[start // size].astype(BF16)
            parts = [parts[2 * i] + parts[2 * i + 1] for i in range(len(parts) // 2)]
            size *= 2
            bit += 1
        total = parts[0].astype(BF16)
        send_s[0, h] = total
        p_s[h] = total.astype(F32)

    states(0)
    load(0, 0).start()
    lam_copy.start()
    pl.semaphore_wait(barrier, bits + head_n - 1)
    send_state(0, 0)

    @pl.loop(1, heads)
    def _(h):
        states(h)
        send_state(0, h)

        load(0, h).start()

    for h in range(AHEAD, heads):
        load(0, h).start()
    for c in range(chunks):
        w_s[c, HALF:C, :HALF] = jnp.zeros((HALF, HALF), BF16)
    lam_copy.wait()
    for h in range(heads):
        lam_s[h] = lam_s[h] * scaling

    lane = lax.broadcasted_iota(jnp.int32, (8, HALF), 1)
    sub = lax.broadcasted_iota(jnp.int32, (8, HALF), 0)
    low = lane & 7
    low_x = low ^ sub
    low_ok = sub <= low
    high = lane >> 3

    def factors(h, start):
        def row(level):
            return lam_s[h, pl.ds(level, 1), pl.ds(start, HALF)]

        def wide(level):
            return jnp.broadcast_to(row(level), (8, HALF))

        fine = jnp.where(low_x < 2, wide(1), jnp.where(low_x < 4, wide(2), wide(3)))
        fine = jnp.where(low_x == 0, wide(0), fine)
        fine = jnp.where(low_ok, fine, 0.0)
        l4, l5, l6, l7 = wide(4), wide(5), wide(6), wide(7)
        pieces = []
        for half in range(2):
            a = sub + 8 * half
            x = a ^ high
            coarse = jnp.where(x < 2, l4, jnp.where(x < 4, l5, jnp.where(x < 8, l6, l7)))
            coarse = jnp.where(a < high, coarse, 0.0)
            for r in range(8):
                spread = jnp.broadcast_to(coarse[r : r + 1, :], (8, HALF))
                pieces.append(jnp.where(high == 8 * half + r, fine, spread))
        return jnp.concatenate(pieces, axis=0)

    def levels_of(c):
        found = []
        for bit in range(chunks.bit_length() - 1):
            if c >> bit & 1:
                found.append((9 + bit, table[(bit, (c >> bit ^ 1) << bit)]))
        return found

    def turn(h, c):
        rows = pl.ds(c * C, C)
        qt = q_s[h, rows, :].T
        qt_s[h, :, rows] = qt
        for i, (level, _) in enumerate(levels_of(c)):
            w_s[c, pl.ds(C + i * D, D), :] = scaled(qt, lam_s[h, pl.ds(level, 1), rows])

    def score(h, c):
        rows = pl.ds(c * C, C)
        prod = nn(k_s[h, rows, :], qt_s[h, :, rows])
        f0 = factors(h, c * C)
        l8 = lam_s[h, pl.ds(8, 1), pl.ds(c * C + HALF, HALF)]
        at = c
        w_s[at, :HALF, :HALF] = (prod[:HALF, :HALF] * f0).astype(BF16)
        w_s[at, :HALF, HALF:] = (prod[:HALF, HALF:] * l8).astype(BF16)
        f1 = factors(h, c * C + HALF)
        w_s[at, HALF:C, HALF:] = (prod[HALF:, HALF:] * f1).astype(BF16)

    def gather(h, c):
        rows = pl.ds(c * C, C)
        lhs = [vt_s[h, :, rows]] + [lv_s[h, slot] for _, slot in levels_of(c)]
        depth = C + D * (len(lhs) - 1)
        acc_s[h, :, rows] = nn(jnp.concatenate(lhs, axis=1), w_s[c, :depth, :])

    def relay(b, h):
        @pl.when(gets[b])
        def _():
            state_copy(b, h).wait_recv()
            if b + 1 < bits:
                @pl.when(sends[b + 1])
                def _():
                    total = p_s[h] + recv_s[h, b].astype(F32)
                    p_s[h] = total
                    send_s[b + 1, h] = total.astype(BF16)
                    state_copy(b + 1, h).start()

    def tick(u):
        for b in range(bits):
            h = u - b * LAG

            @pl.when(jnp.logical_and(h >= 0, h < heads))
            def _():
                relay(b, h)

    def due(step):
        return step * RATE // 3

    sq_s[...] = jnp.zeros_like(sq_s)
    for b in range(bits):
        @pl.when(jnp.logical_not(gets[b]))
        def _():
            for h in range(heads):
                recv_s[h, b] = jnp.zeros((E, D), BF16)


    @pl.loop(0, heads)
    def _(h):
        pl.loop(due(jnp.maximum(h - 1, 0)), due(h))(tick)
        load(0, h).wait()
        for c in range(chunks):
            turn(h, c)
        for c in range(chunks):
            score(h, c)
        for c in range(chunks):
            gather(h, c)

    on = [(lax.shift_right_logical(me_seq, b) & 1).astype(F32) for b in range(bits)]

    def across(h):
        def spread(c):
            rows = pl.ds(c * C, C)
            qt = qt_s[h, :, rows]
            for b in range(bits):
                weight = lam_s[h, pl.ds(local_bits + 1 + b, 1), rows] * on[b]
                x_s[c, pl.ds(b * D, D), :] = scaled(qt, weight)

        def read(c):
            rows = pl.ds(c * C, C)
            lhs = jnp.concatenate([recv_s[h, b] for b in range(bits)], axis=1)
            acc = acc_s[h, :, rows] + nn(lhs, x_s[c])
            acc_s[h, :, rows] = acc
            sq = acc * acc
            square = sq_s[:, rows]
            for r in range(E // 8):
                square = square + sq[r * 8 : (r + 1) * 8]
            sq_s[:, rows] = square

        for c in range(chunks):
            spread(c)
        for c in range(chunks):
            read(c)

    last = (bits - 1) * LAG

    @pl.loop(min(due(heads - 1), last), heads + last)
    def _(u):
        @pl.when(u >= due(heads - 1))
        def _():
            tick(u)

        @pl.when(u >= last)
        def _():
            across(u - last)

    sqx_s[me_head] = jnp.sum(sq_s[...], axis=0, keepdims=True)

    def sq_copy(k):
        return pltpu.make_async_remote_copy(
            src_ref=sqx_s.at[me_head],
            dst_ref=sqx_s.at[me_head],
            send_sem=sq_send_sem.at[k],
            recv_sem=sq_recv_sem.at[k],
            device_id={"head": lax.rem(me_head + k, head_n)},
            device_id_type=MESH,
        )

    def sq_arrive(k):
        owner = lax.rem(me_head + head_n - k, head_n)
        return pltpu.make_async_remote_copy(
            src_ref=sqx_s.at[owner],
            dst_ref=sqx_s.at[owner],
            send_sem=sq_send_sem.at[k],
            recv_sem=sq_recv_sem.at[k],
            device_id={"head": lax.rem(me_head + k, head_n)},
            device_id_type=MESH,
        )

    for k in sorted(range(1, head_n), key=lambda k: abs(k - head_n // 2)):
        sq_copy(k).start()

    @pl.loop(0, heads)
    def _(h):
        cols = pl.ds(pl.multiple_of(h * E, E), E)
        for c in range(chunks):
            rows = pl.ds(c * C, C)
            out_ref[rows, cols] = acc_s[h, :, rows].T * gain_ref[pl.ds(h, 1), :]

    @pl.loop(0, heads)
    def _(h):
        for b in range(bits):
            @pl.when(sends[b])
            def _():
                state_copy(b, h).wait_send()

    for k in range(1, head_n):
        sq_arrive(k).wait_recv()
    total = sqx_s[0]
    for k in range(1, head_n):
        total = total + sqx_s[k]
    scale_ref[...] = lax.rsqrt(total / (HEADS * E) + 1e-05)

    for k in range(1, head_n):
        sq_copy(k).wait_send()


def finish(tokens, acc_ref, scale_ref, out_hbm, buf, col_s, sem):
    def out_copy(i):
        rows = pl.ds(i * HALF, HALF)
        return pltpu.make_async_copy(buf.at[i], out_hbm.at[rows, :], sem.at[i])

    def turn(i):
        rows = pl.ds(i * HALF, HALF)
        col_s[rows, :] = jnp.broadcast_to(scale_ref[:, rows], (HALF, HALF)).T

    blocks = tokens // HALF
    turn(0)
    for i in range(blocks):
        if i + 1 < blocks:
            turn(i + 1)
        rows = pl.ds(i * HALF, HALF)
        for h in range(acc_ref.shape[1] // E):
            cols = pl.ds(h * E, E)
            buf[i, :, cols] = (acc_ref[rows, cols] * col_s[rows, :]).astype(BF16)
        out_copy(i).start()
    for i in range(blocks):
        out_copy(i).wait()


def body(queries, key_vectors, value_vectors, level_weights, norm_gain):
    tokens = queries.shape[0]
    heads, levels = level_weights.shape[:2]
    seq_n = lax.axis_size("seq")
    head_n = lax.axis_size("head")
    bits = seq_n.bit_length() - 1
    slots = max(len(buckets_of(tokens // C)), 1)
    any_spec = pl.BlockSpec(memory_space=pl.ANY)
    vmem = pl.BlockSpec(memory_space=pltpu.VMEM)
    mixture, scale = pl.pallas_call(
        functools.partial(kernel, seq_n, head_n, heads, tokens),
        out_shape=(pltpu.VMEM((tokens, heads * E), F32), pltpu.VMEM((1, tokens), F32)),
        in_specs=[pl.BlockSpec(memory_space=pltpu.HBM)] * 4 + [vmem],
        out_specs=(vmem, vmem),
        scratch_shapes=[
            pltpu.VMEM((heads, tokens, D), BF16),
            pltpu.VMEM((heads, tokens, D), BF16),
            pltpu.VMEM((heads, tokens, E), BF16),
            pltpu.VMEM((heads, levels, tokens), F32),
            pltpu.VMEM((heads, E, tokens), BF16),
            pltpu.VMEM((heads, E, tokens), F32),
            pltpu.VMEM((heads, slots, E, D), BF16),
            pltpu.VMEM((heads, E, D), F32),
            pltpu.VMEM((bits, heads, E, D), BF16),
            pltpu.VMEM((heads, bits, E, D), BF16),
            pltpu.VMEM((8, tokens), F32),
            pltpu.VMEM((head_n, 1, tokens), F32),
            pltpu.VMEM((tokens // C, C + 3 * D, C), BF16),
            pltpu.VMEM((heads, D, tokens), BF16),
            pltpu.VMEM((tokens // C, bits * D, C), BF16),
            pltpu.SemaphoreType.DMA((3, heads)),
            pltpu.SemaphoreType.DMA,
            pltpu.SemaphoreType.DMA((bits, heads)),
            pltpu.SemaphoreType.DMA((bits, heads)),
            pltpu.SemaphoreType.DMA((head_n,)),
            pltpu.SemaphoreType.DMA((head_n,)),
        ],
        compiler_params=pltpu.CompilerParams(
            collective_id=0, has_side_effects=True, vmem_limit_bytes=58 * 1000 * 1000
        ),
        name="fenwick",
    )(queries, key_vectors, value_vectors, level_weights, norm_gain.reshape(heads, E))
    return pl.pallas_call(
        functools.partial(finish, tokens),
        out_shape=jax.ShapeDtypeStruct((tokens, heads * E), BF16),
        in_specs=[vmem, vmem],
        out_specs=any_spec,
        scratch_shapes=[
            pltpu.VMEM((tokens // HALF, HALF, heads * E), BF16),
            pltpu.VMEM((tokens, HALF), F32),
            pltpu.SemaphoreType.DMA((tokens // HALF,)),
        ],
        compiler_params=pltpu.CompilerParams(vmem_limit_bytes=16 * 1024 * 1024),
        name="finish",
    )(mixture, scale)


def solution(mesh):
    placed = (
        P("seq", "head"),
        P("seq", "head"),
        P("seq", "head"),
        P("head", None, "seq"),
        P("head"),
    )
    return jax.shard_map(
        body, mesh=mesh, in_specs=placed, out_specs=P("seq", "head"), check_vma=False
    )
```

```python
import functools

import jax
import jax.numpy as jnp
from jax import lax
from jax.experimental import pallas as pl
from jax.experimental.pallas import tpu as pltpu
from jax.sharding import PartitionSpec as P

D = 128
E = 128
C = 256
HALF = 128
HEADS = 64
LAG = 4
RATE = 4
AHEAD = 8
MESH = pl.DeviceIdType.MESH
F32 = jnp.float32
BF16 = jnp.bfloat16


def nt(a, b):
    return lax.dot_general(a, b, (((1,), (1,)), ((), ())), preferred_element_type=F32)


def nn(a, b):
    return lax.dot_general(a, b, (((1,), (0,)), ((), ())), preferred_element_type=F32)


def partner_mask(bit):
    return 1 << bit if bit % 2 == 0 else 3 << (bit - 1)


def scaled(qt, row):
    width = qt.shape[1]
    weight = jnp.broadcast_to(row, (16, width)).astype(BF16)
    return qt * jnp.concatenate([weight] * (qt.shape[0] // 16), axis=0)


def buckets_of(chunks):
    table = {}
    bit = 0
    while 1 << bit < chunks:
        for start in range(0, chunks, 2 << bit):
            table[(bit, start)] = len(table)
        bit += 1
    return table


def kernel(
    seq_n, head_n, heads, tokens,
    q_hbm, k_hbm, v_hbm, lam_hbm, gain_ref,
    out_ref, scale_ref,
    q_s, k_s, v_s, lam_s, vt_s, acc_s, lv_s, p_s, send_s, recv_s, sq_s, sqx_s, w_s, qt_s, x_s,
    load_sem, lam_sem, send_sem, recv_sem, sq_send_sem, sq_recv_sem,
):
    chunks = tokens // C
    bits = seq_n.bit_length() - 1
    local_bits = tokens.bit_length() - 1
    me_seq = lax.axis_index("seq")
    me_head = lax.axis_index("head")
    table = buckets_of(chunks)
    scaling = D ** (-0.5)

    def load(which, h):
        src, dst = ((q_hbm, q_s), (k_hbm, k_s), (v_hbm, v_s))[which]
        cols = pl.ds(pl.multiple_of(h * D, D), D)
        return pltpu.make_async_copy(src.at[:, cols], dst.at[h], load_sem.at[which, h])

    lam_copy = pltpu.make_async_copy(lam_hbm, lam_s, lam_sem)

    barrier = pltpu.get_barrier_semaphore()
    for k in sorted(range(1, head_n), key=lambda k: abs(k - head_n // 2)):
        pl.semaphore_signal(
            barrier, inc=1, device_id={"head": lax.rem(me_head + k, head_n)}, device_id_type=MESH
        )

    for h in range(AHEAD):
        load(2, h).start()
        load(1, h).start()

    for b in range(bits):
        pl.semaphore_signal(
            barrier, inc=1, device_id={"seq": me_seq ^ partner_mask(b)}, device_id_type=MESH
        )

    def state_copy(b, h):
        return pltpu.make_async_remote_copy(
            src_ref=send_s.at[b, h],
            dst_ref=recv_s.at[h, b],
            send_sem=send_sem.at[b, h],
            recv_sem=recv_sem.at[b, h],
            device_id={"seq": me_seq ^ partner_mask(b)},
            device_id_type=MESH,
        )

    sends = [me_seq < seq_n - (1 << b) for b in range(bits)]
    gets = [(me_seq ^ partner_mask(b)) < seq_n - (1 << b) for b in range(bits)]

    def send_state(b, h):
        @pl.when(sends[b])
        def _():
            state_copy(b, h).start()

    def states(h):
        load(2, h).wait()
        load(1, h).wait()
        parts = []
        for c in range(chunks):
            rows = pl.ds(c * C, C)
            vt = v_s[h, rows, :].T
            vt_s[h, :, pl.ds(c * C, C)] = vt
            parts.append(nn(vt, k_s[h, rows, :]))
        size = 1
        bit = 0
        while size < chunks:
            for start in range(0, chunks, 2 * size):
                lv_s[h, table[(bit, start)]] = parts[start // size].astype(BF16)
            parts = [parts[2 * i] + parts[2 * i + 1] for i in range(len(parts) // 2)]
            size *= 2
            bit += 1
        total = parts[0].astype(BF16)
        send_s[0, h] = total
        p_s[h] = total.astype(F32)

    states(0)
    load(0, 0).start()
    lam_copy.start()
    pl.semaphore_wait(barrier, bits + head_n - 1)
    send_state(0, 0)

    @pl.loop(1, heads)
    def _(h):
        states(h)
        send_state(0, h)

        load(0, h).start()

    for h in range(AHEAD, heads):
        load(0, h).start()
    for c in range(chunks):
        w_s[c, HALF:C, :HALF] = jnp.zeros((HALF, HALF), BF16)
    lam_copy.wait()
    for h in range(heads):
        lam_s[h] = lam_s[h] * scaling

    lane = lax.broadcasted_iota(jnp.int32, (8, HALF), 1)
    sub = lax.broadcasted_iota(jnp.int32, (8, HALF), 0)
    low = lane & 7
    low_x = low ^ sub
    low_ok = sub <= low
    high = lane >> 3

    def factors(h, start):
        def row(level):
            return lam_s[h, pl.ds(level, 1), pl.ds(start, HALF)]

        def wide(level):
            return jnp.broadcast_to(row(level), (8, HALF))

        fine = jnp.where(low_x < 2, wide(1), jnp.where(low_x < 4, wide(2), wide(3)))
        fine = jnp.where(low_x == 0, wide(0), fine)
        fine = jnp.where(low_ok, fine, 0.0)
        l4, l5, l6, l7 = wide(4), wide(5), wide(6), wide(7)
        pieces = []
        for half in range(2):
            a = sub + 8 * half
            x = a ^ high
            coarse = jnp.where(x < 2, l4, jnp.where(x < 4, l5, jnp.where(x < 8, l6, l7)))
            coarse = jnp.where(a < high, coarse, 0.0)
            for r in range(8):
                spread = jnp.broadcast_to(coarse[r : r + 1, :], (8, HALF))
                pieces.append(jnp.where(high == 8 * half + r, fine, spread))
        return jnp.concatenate(pieces, axis=0)

    def levels_of(c):
        found = []
        for bit in range(chunks.bit_length() - 1):
            if c >> bit & 1:
                found.append((9 + bit, table[(bit, (c >> bit ^ 1) << bit)]))
        return found

    def turn(h, c):
        rows = pl.ds(c * C, C)
        qt = q_s[h, rows, :].T
        qt_s[h, :, rows] = qt
        for i, (level, _) in enumerate(levels_of(c)):
            w_s[c, pl.ds(C + i * D, D), :] = scaled(qt, lam_s[h, pl.ds(level, 1), rows])

    def score(h, c):
        rows = pl.ds(c * C, C)
        prod = nn(k_s[h, rows, :], qt_s[h, :, rows])
        f0 = factors(h, c * C)
        l8 = lam_s[h, pl.ds(8, 1), pl.ds(c * C + HALF, HALF)]
        at = c
        w_s[at, :HALF, :HALF] = (prod[:HALF, :HALF] * f0).astype(BF16)
        w_s[at, :HALF, HALF:] = (prod[:HALF, HALF:] * l8).astype(BF16)
        f1 = factors(h, c * C + HALF)
        w_s[at, HALF:C, HALF:] = (prod[HALF:, HALF:] * f1).astype(BF16)

    def gather(h, c):
        rows = pl.ds(c * C, C)
        lhs = [vt_s[h, :, rows]] + [lv_s[h, slot] for _, slot in levels_of(c)]
        depth = C + D * (len(lhs) - 1)
        acc_s[h, :, rows] = nn(jnp.concatenate(lhs, axis=1), w_s[c, :depth, :])

    def relay(b, h):
        @pl.when(gets[b])
        def _():
            state_copy(b, h).wait_recv()
            if b + 1 < bits:
                @pl.when(sends[b + 1])
                def _():
                    total = p_s[h] + recv_s[h, b].astype(F32)
                    p_s[h] = total
                    send_s[b + 1, h] = total.astype(BF16)
                    state_copy(b + 1, h).start()

    def tick(u):
        for b in range(bits):
            h = u - b * LAG

            @pl.when(jnp.logical_and(h >= 0, h < heads))
            def _():
                relay(b, h)

    def due(step):
        return (step * RATE + 2) // 3

    sq_s[...] = jnp.zeros_like(sq_s)
    for b in range(bits):
        @pl.when(jnp.logical_not(gets[b]))
        def _():
            for h in range(heads):
                recv_s[h, b] = jnp.zeros((E, D), BF16)


    @pl.loop(0, heads)
    def _(h):
        pl.loop(due(jnp.maximum(h - 1, 0)), due(h))(tick)
        load(0, h).wait()
        for c in range(chunks):
            turn(h, c)
        for c in range(chunks):
            score(h, c)
        for c in range(chunks):
            gather(h, c)

    on = [(lax.shift_right_logical(me_seq, b) & 1).astype(F32) for b in range(bits)]

    def across(h):
        def spread(c):
            rows = pl.ds(c * C, C)
            qt = qt_s[h, :, rows]
            for b in range(bits):
                weight = lam_s[h, pl.ds(local_bits + 1 + b, 1), rows] * on[b]
                x_s[c, pl.ds(b * D, D), :] = scaled(qt, weight)

        def read(c):
            rows = pl.ds(c * C, C)
            lhs = jnp.concatenate([recv_s[h, b] for b in range(bits)], axis=1)
            acc = acc_s[h, :, rows] + nn(lhs, x_s[c])
            acc_s[h, :, rows] = acc
            sq = acc * acc
            square = sq_s[:, rows]
            for r in range(E // 8):
                square = square + sq[r * 8 : (r + 1) * 8]
            sq_s[:, rows] = square

        for c in range(chunks):
            spread(c)
        for c in range(chunks):
            read(c)

    last = (bits - 1) * LAG

    @pl.loop(min(due(heads - 1), last), heads + last)
    def _(u):
        @pl.when(u >= due(heads - 1))
        def _():
            tick(u)

        @pl.when(u >= last)
        def _():
            across(u - last)

    sqx_s[me_head] = jnp.sum(sq_s[...], axis=0, keepdims=True)

    def sq_copy(k):
        return pltpu.make_async_remote_copy(
            src_ref=sqx_s.at[me_head],
            dst_ref=sqx_s.at[me_head],
            send_sem=sq_send_sem.at[k],
            recv_sem=sq_recv_sem.at[k],
            device_id={"head": lax.rem(me_head + k, head_n)},
            device_id_type=MESH,
        )

    def sq_arrive(k):
        owner = lax.rem(me_head + head_n - k, head_n)
        return pltpu.make_async_remote_copy(
            src_ref=sqx_s.at[owner],
            dst_ref=sqx_s.at[owner],
            send_sem=sq_send_sem.at[k],
            recv_sem=sq_recv_sem.at[k],
            device_id={"head": lax.rem(me_head + k, head_n)},
            device_id_type=MESH,
        )

    for k in sorted(range(1, head_n), key=lambda k: abs(k - head_n // 2)):
        sq_copy(k).start()

    @pl.loop(0, heads)
    def _(h):
        cols = pl.ds(pl.multiple_of(h * E, E), E)
        for c in range(chunks):
            rows = pl.ds(c * C, C)
            out_ref[rows, cols] = acc_s[h, :, rows].T * gain_ref[pl.ds(h, 1), :]

    @pl.loop(0, heads)
    def _(h):
        for b in range(bits):
            @pl.when(sends[b])
            def _():
                state_copy(b, h).wait_send()

    for k in range(1, head_n):
        sq_arrive(k).wait_recv()
    total = sqx_s[0]
    for k in range(1, head_n):
        total = total + sqx_s[k]
    scale_ref[...] = lax.rsqrt(total / (HEADS * E) + 1e-05)

    for k in range(1, head_n):
        sq_copy(k).wait_send()


def finish(tokens, acc_ref, scale_ref, out_hbm, buf, col_s, sem):
    def out_copy(i):
        rows = pl.ds(i * HALF, HALF)
        return pltpu.make_async_copy(buf.at[i], out_hbm.at[rows, :], sem.at[i])

    def turn(i):
        rows = pl.ds(i * HALF, HALF)
        col_s[rows, :] = jnp.broadcast_to(scale_ref[:, rows], (HALF, HALF)).T

    blocks = tokens // HALF
    turn(0)
    for i in range(blocks):
        if i + 1 < blocks:
            turn(i + 1)
        rows = pl.ds(i * HALF, HALF)
        for h in range(acc_ref.shape[1] // E):
            cols = pl.ds(h * E, E)
            buf[i, :, cols] = (acc_ref[rows, cols] * col_s[rows, :]).astype(BF16)
        out_copy(i).start()
    for i in range(blocks):
        out_copy(i).wait()


def body(queries, key_vectors, value_vectors, level_weights, norm_gain):
    tokens = queries.shape[0]
    heads, levels = level_weights.shape[:2]
    seq_n = lax.axis_size("seq")
    head_n = lax.axis_size("head")
    bits = seq_n.bit_length() - 1
    slots = max(len(buckets_of(tokens // C)), 1)
    any_spec = pl.BlockSpec(memory_space=pl.ANY)
    vmem = pl.BlockSpec(memory_space=pltpu.VMEM)
    mixture, scale = pl.pallas_call(
        functools.partial(kernel, seq_n, head_n, heads, tokens),
        out_shape=(pltpu.VMEM((tokens, heads * E), F32), pltpu.VMEM((1, tokens), F32)),
        in_specs=[pl.BlockSpec(memory_space=pltpu.HBM)] * 4 + [vmem],
        out_specs=(vmem, vmem),
        scratch_shapes=[
            pltpu.VMEM((heads, tokens, D), BF16),
            pltpu.VMEM((heads, tokens, D), BF16),
            pltpu.VMEM((heads, tokens, E), BF16),
            pltpu.VMEM((heads, levels, tokens), F32),
            pltpu.VMEM((heads, E, tokens), BF16),
            pltpu.VMEM((heads, E, tokens), F32),
            pltpu.VMEM((heads, slots, E, D), BF16),
            pltpu.VMEM((heads, E, D), F32),
            pltpu.VMEM((bits, heads, E, D), BF16),
            pltpu.VMEM((heads, bits, E, D), BF16),
            pltpu.VMEM((8, tokens), F32),
            pltpu.VMEM((head_n, 1, tokens), F32),
            pltpu.VMEM((tokens // C, C + 3 * D, C), BF16),
            pltpu.VMEM((heads, D, tokens), BF16),
            pltpu.VMEM((tokens // C, bits * D, C), BF16),
            pltpu.SemaphoreType.DMA((3, heads)),
            pltpu.SemaphoreType.DMA,
            pltpu.SemaphoreType.DMA((bits, heads)),
            pltpu.SemaphoreType.DMA((bits, heads)),
            pltpu.SemaphoreType.DMA((head_n,)),
            pltpu.SemaphoreType.DMA((head_n,)),
        ],
        compiler_params=pltpu.CompilerParams(
            collective_id=0, has_side_effects=True, vmem_limit_bytes=58 * 1000 * 1000
        ),
        name="fenwick",
    )(queries, key_vectors, value_vectors, level_weights, norm_gain.reshape(heads, E))
    return pl.pallas_call(
        functools.partial(finish, tokens),
        out_shape=jax.ShapeDtypeStruct((tokens, heads * E), BF16),
        in_specs=[vmem, vmem],
        out_specs=any_spec,
        scratch_shapes=[
            pltpu.VMEM((tokens // HALF, HALF, heads * E), BF16),
            pltpu.VMEM((tokens, HALF), F32),
            pltpu.SemaphoreType.DMA((tokens // HALF,)),
        ],
        compiler_params=pltpu.CompilerParams(vmem_limit_bytes=16 * 1024 * 1024),
        name="finish",
    )(mixture, scale)


def solution(mesh):
    placed = (
        P("seq", "head"),
        P("seq", "head"),
        P("seq", "head"),
        P("head", None, "seq"),
        P("head"),
    )
    return jax.shard_map(
        body, mesh=mesh, in_specs=placed, out_specs=P("seq", "head"), check_vma=False
    )
```
